32 devices in a mesh: groups: 2 (over x), ep: 16 (over z, y, core).
Axes of the slice: x: 2, y: 2, z: 4, core: 2. Of those that a mesh axis runs over, the one named last changes fastest.
Arguments:
- inputs: float32 [64, 6144], P(('groups', 'ep')), parts along dimension 0, may hold values from -6 to 6
- norm_gain: float32 [6144], replicated, may hold values from 0.5 to 1.5
- dense_gate: bfloat16 [6144, 12288], P(None, 'ep'), may hold values from -0.078125 to 0.078125
- dense_up: bfloat16 [6144, 12288], P(None, 'ep'), may hold values from -0.078125 to 0.078125
- dense_down: bfloat16 [12288, 6144], P('ep'), may hold values from -0.0546875 to 0.0546875
- expert_gate: bfloat16 [6144, 32768], P(None, 'ep'), may hold values from -0.078125 to 0.078125
- expert_up: bfloat16 [6144, 32768], P(None, 'ep'), may hold values from -0.078125 to 0.078125
- expert_down: bfloat16 [32768, 6144], P('ep'), may hold values from -0.125 to 0.125
- expert_ids: int32 [64, 12], P('groups'), parts along dimension 0, may hold values from 0 to 16, all different within a row; in each aligned block of 2 rows (0 to 1, 2 to 3, ...) at most 2 rows name the same one
- route_weights: int32 [64, 12], P('groups'), parts along dimension 0, may hold values from 1 to 1024
- out_gain: float32 [6144], replicated, may hold values from 0.5 to 1.5
Outputs:
- result: float32 [64, 6144], P(('groups', 'ep')), parts along dimension 0
The draws below stay inside these ranges and needn't reach their ends.
There are 2 independent parts, one for each index of `groups`. The reference program is written for one: setup_inputs(seed, part) draws one part's arguments, and reference() takes and returns one part's arrays. A program takes and returns all parts, laid end to end along the dimension named above; an argument that names none is the same for every part. Nothing has to cross between parts.
Inputs may be any that keep to these rules, and one draw needn't show every extreme that they name: `expert_ids`: each row names 12 different values; in the rows of one device (aligned blocks of 2 rows) no value is named by more than 2 rows, and in every draw some value is named by exactly 2 rows of one device.
All inputs are finite; a program needn't handle non-finite values.
Results may differ from the reference program's by a relative error of at most 0.0031.
Values may be sent and summed in bfloat16 or wider, within the bound.
A program may use at most 192 MiB of HBM per device.

```python
import math
import jax
import jax.numpy as jnp
import numpy as np
from jax import lax

D = 6144
FF = 12288
EF = 2048
EXPERTS = 16
TOPK = 12
ROWS_DEV = 2
MOST = 2
TOKENS = 32
N_EP = 16


def with_ends(array, rng, smallest, high):
    extent = array.shape
    spot = [jax.random.randint(jax.random.fold_in(rng, axis), (), 0, extent[axis]) for axis in range(len(extent))]
    array = array.at[tuple(spot)].set(smallest)
    longest = extent.index(max(extent))
    spot[longest] = (spot[longest] + 1) % extent[longest]
    return array.at[tuple(spot)].set(high)


def steps_of(rng, extent, pieces, low, largest):
    level, own = 1.0, jax.random.fold_in(rng, 6)
    for dim, blocks in pieces:
        steps = jnp.exp(jax.random.uniform(jax.random.fold_in(own, dim), (blocks,), jnp.float32, low / len(pieces), largest / len(pieces)))
        level = level * jnp.repeat(steps, extent[dim] // blocks).reshape([-1 if axis == dim else 1 for axis in range(len(extent))])
    return level


def shared_out(key, own, number, rows, number_of, top, reach, slope):
    sequence = jax.random.permutation(key, number_of)
    crowded, ordinary = portions_of(number_of, rows * top, reach, slope, True), portions_of(number_of, rows * top, reach, slope, False)
    places = jnp.arange(number_of)

    def named(lengths, turn):
        used = int((lengths > 0).sum())
        fixed = max(1, used // 4)
        moved = fixed + (places - fixed + turn * (used - fixed)) % max(1, number_of - fixed)
        return jnp.zeros((number_of,), jnp.int32).at[sequence[jnp.where(places < fixed, places, moved)]].set(jnp.asarray(lengths, jnp.int32))

    lengths = jnp.where(number % 4 == 0, named(crowded, number // 4), named(ordinary, number - number // 4 - 1))
    mixed = jax.random.permutation(jax.random.fold_in(own, 3), number_of)
    source_of, taker = mixed[0:number_of // 2 * 2:2], mixed[1:number_of // 2 * 2:2]
    slack = jnp.minimum(lengths[source_of] - 1, reach - lengths[taker]) // 2
    slack = jnp.where((source_of == sequence[0]) | (taker == sequence[0]) | (lengths[taker] == 0), 0, jnp.maximum(slack, 0))
    moved = jax.random.randint(jax.random.fold_in(own, 4), (number_of // 2,), 0, 1 << 20) % (slack + 1)
    lengths = lengths.at[source_of].add(-moved).at[taker].add(moved)
    members = jnp.searchsorted(jnp.cumsum(lengths), jnp.arange(rows * top), side="right").astype(jnp.int32)
    table = members.reshape(top, rows).T
    table = table[jax.random.permutation(jax.random.fold_in(own, 1), rows)]
    turn = jax.random.randint(jax.random.fold_in(own, 2), (rows, 1), 0, top)
    return jnp.take_along_axis(table, (jnp.arange(top)[None, :] + turn) % top, axis=1)


def portions_of(count, total, limit, slope, full):
    portions = [(1 << 20) // math.isqrt(standing ** slope) + 1 for standing in range(1, count + 1)]
    largest = limit if full else min(limit, max(-(-total // count), total * portions[0] // sum(portions)))
    least = 1 if total - largest >= count - 1 else 0
    counts, rest = [largest] + [least] * (count - 1), total - largest - least * (count - 1)
    while rest > 0:
        free = [i for i in range(1, count) if counts[i] < largest] or [i for i in range(1, count) if counts[i] < limit]
        mass, left = sum([portions[i] for i in free]), rest
        for i in free:
            more = min(limit - counts[i], max(1, left * portions[i] // mass), rest)
            counts[i] = counts[i] + more
            rest = rest - more
    return np.array(counts)


def bell_draw(key, extent, scale, reach, split=(), kind=jnp.bfloat16):
    drawn = jax.random.normal(key, extent, jnp.float32) * scale
    if len(split) > 0:
        drawn = steps_of(key, extent, split, -0.22, 0.18) * drawn
    return jnp.clip(drawn, min=-reach, max=reach).astype(kind)


def setup_inputs(seed: int = 0, part: int = 0) -> dict:
    splits = jax.random.split(jax.random.key(seed), 12)
    part_splits = jax.random.split(jax.random.fold_in(splits[11], part), 12)
    inputs = bell_draw(part_splits[0], (TOKENS, D), 1.0, 6.0, ((0, 16),), jnp.float32)
    norm_gain = jnp.clip(1.0 + 0.1 * jax.random.normal(splits[1], (D,), jnp.float32), 0.5, 1.5)
    dense_gate = bell_draw(splits[2], (D, FF), D ** -0.5, 0.078125, ((1, 16),))
    dense_up = bell_draw(splits[3], (D, FF), D ** -0.5, 0.078125, ((1, 16),))
    dense_down = bell_draw(splits[4], (FF, D), FF ** -0.5, 0.0546875, ((0, 16),))
    expert_gate = bell_draw(splits[5], (D, EXPERTS * EF), D ** -0.5, 0.078125, ((1, 16),))
    expert_up = bell_draw(splits[6], (D, EXPERTS * EF), D ** -0.5, 0.078125, ((1, 16),))
    expert_down = bell_draw(splits[7], (EXPERTS * EF, D), EF ** -0.5, 0.125, ((0, 16),))
    expert_ids_keys = jax.random.split(jax.random.fold_in(part_splits[8], 1), TOKENS // ROWS_DEV)
    expert_ids_turns = jax.random.permutation(jax.random.fold_in(part_splits[8], 3), TOKENS // ROWS_DEV)
    expert_ids = jax.vmap(lambda own, number: shared_out(jax.random.fold_in(part_splits[8], 2), own, number, ROWS_DEV, EXPERTS + 1, TOPK, MOST, 1))(expert_ids_keys, expert_ids_turns).reshape((TOKENS, TOPK))
    route_weights = with_ends(jax.random.randint(part_splits[9], (TOKENS, TOPK), 1, 1025), jax.random.fold_in(part_splits[9], 1), 1, 1024).astype(jnp.int32)
    out_gain = jnp.clip(1.0 + 0.1 * jax.random.normal(splits[10], (D,), jnp.float32), 0.5, 1.5)
    return dict(inputs=inputs, norm_gain=norm_gain, dense_gate=dense_gate, dense_up=dense_up, dense_down=dense_down, expert_gate=expert_gate, expert_up=expert_up, expert_down=expert_down, expert_ids=expert_ids, route_weights=route_weights, out_gain=out_gain)


def rms_scale(values):
    return values * lax.rsqrt(lax.optimization_barrier(jnp.mean(values * values, axis=-1, keepdims=True)) + 1e-06)

def slot_table(expert_ids, weights_all, expert, blocks, block_rows):
    matches = expert_ids == expert
    picked = jnp.any(matches, axis=1).reshape(blocks, block_rows)
    weight = lax.optimization_barrier(jnp.sum(jnp.where(matches, weights_all, 0.0), axis=1)).reshape(blocks, block_rows)
    ranking = jnp.cumsum(picked.astype(jnp.int32), axis=1) - 1
    position = lax.broadcasted_iota(jnp.int32, (blocks, block_rows), 1)
    row_cols = []
    weight_cols = []
    for column in range(MOST):
        chosen = picked & (ranking == column)
        row_cols.append(lax.optimization_barrier(jnp.sum(jnp.where(chosen, position, 0), axis=1)).astype(jnp.int32))
        weight_cols.append(lax.optimization_barrier(jnp.sum(jnp.where(chosen, weight, 0.0), axis=1)))
    offsets = (lax.broadcasted_iota(jnp.int32, (blocks, 1), 0) * block_rows).astype(jnp.int32)
    slot_rows = (jnp.stack(row_cols, axis=1) + offsets).reshape(-1).astype(jnp.int32)
    slot_weight = jnp.stack(weight_cols, axis=1).reshape(-1)
    return (slot_rows, slot_weight)

def reference(inputs, norm_gain, dense_gate, dense_up, dense_down, expert_gate, expert_up, expert_down, expert_ids, route_weights, out_gain):
    hidden_in = (rms_scale(inputs) * norm_gain).astype(jnp.bfloat16)
    gate = jnp.dot(hidden_in, dense_gate, preferred_element_type=jnp.float32)
    upper = jnp.dot(hidden_in, dense_up, preferred_element_type=jnp.float32)
    dense_hidden = (jax.nn.silu(gate) * upper).astype(jnp.bfloat16)
    dense = jnp.dot(dense_hidden, dense_down, preferred_element_type=jnp.float32)
    weights_all = route_weights.astype(jnp.float32) / 1024.0
    zero_weight = lax.optimization_barrier(jnp.sum(jnp.where(expert_ids == EXPERTS, weights_all, 0.0), axis=1))
    start_moe = zero_weight[:, None] * hidden_in.astype(jnp.float32)

    def add_expert(expert, moe):
        slot_rows, slot_weight = slot_table(expert_ids, weights_all, expert, N_EP, ROWS_DEV)
        picked_in = hidden_in[slot_rows]
        column = (expert * EF).astype(jnp.int32)
        w_gate = lax.dynamic_slice_in_dim(expert_gate, column, EF, 1)
        w_upper = lax.dynamic_slice_in_dim(expert_up, column, EF, 1)
        w_down = lax.dynamic_slice_in_dim(expert_down, column, EF, 0)
        e_gate = jnp.dot(picked_in, w_gate, preferred_element_type=jnp.float32)
        e_upper = jnp.dot(picked_in, w_upper, preferred_element_type=jnp.float32)
        e_hidden = (jax.nn.silu(e_gate) * e_upper).astype(jnp.bfloat16)
        outcome = jnp.dot(e_hidden, w_down, preferred_element_type=jnp.float32) * slot_weight[:, None]
        return moe.at[slot_rows].add(outcome)
    moe = lax.fori_loop(0, EXPERTS, add_expert, start_moe)
    joined = dense + moe
    return inputs + rms_scale(joined) * out_gain
```

```python
import functools

import jax
import jax.numpy as jnp
from jax import lax
from jax.experimental import pallas as pl
from jax.experimental.pallas import tpu as pltpu
from jax.sharding import PartitionSpec as P

EXPERTS = 16
WIDE = 256
QUARTERS = 4
VMEM_TOTAL = 66_900_000


def kernel(
    cfg,
    inputs_hbm,
    norm_gain_hbm,
    dense_gate,
    dense_up,
    dense_down,
    expert_gate,
    expert_up,
    expert_down,
    ids_hbm,
    route_hbm,
    out_gain_hbm,
    out_ref,
    inputs,
    norm_gain,
    out_gain,
    ids,
    route,
    ring,
    spare,
    landed,
    rows_in,
    dense_hidden,
    expert_hidden,
    by_device,
    scale,
    outgoing,
    incoming,
    small_sem,
    ring_sem,
    spare_sem,
    gather_send,
    gather_recv,
    reduce_send,
    reduce_recv,
):
    n, own, slots, n_dense, n_expert, n_down = cfg
    rows = n * own
    width = inputs.shape[1]
    k_dense = dense_down.shape[0]
    k_expert = expert_down.shape[0]
    k_both = k_dense + k_expert
    n_up = n_dense + n_expert
    total = n_up + n_down
    me = lax.axis_index("ep")
    expert = me // (n // EXPERTS)

    def up_copies(unit, first, gate, upper):
        slot = lax.rem(unit, slots)
        columns = pl.ds(pl.multiple_of((unit - first) * WIDE, WIDE), WIDE)
        return [
            pltpu.make_async_copy(
                source.at[:, columns], ring.at[slot, which], ring_sem.at[slot, which]
            )
            for which, source in enumerate((gate, upper))
        ]

    def down_copies(unit, quarter):
        slot = lax.rem(unit, slots)
        start = ((unit - n_up) * QUARTERS + quarter) * WIDE
        columns = pl.ds(pl.multiple_of(start, WIDE), WIDE)
        base = (quarter % 2) * k_both
        return [
            pltpu.make_async_copy(
                dense_down.at[:, columns],
                ring.at[slot, quarter // 2, pl.ds(base, k_dense)],
                ring_sem.at[slot, 2 * quarter],
            ),
            pltpu.make_async_copy(
                expert_down.at[:, columns],
                ring.at[slot, quarter // 2, pl.ds(base + k_dense, k_expert)],
                ring_sem.at[slot, 2 * quarter + 1],
            ),
        ]

    def start_unit(unit):
        @pl.when(unit < n_dense)
        def _():
            for copy in up_copies(unit, 0, dense_gate, dense_up):
                copy.start()

        @pl.when((unit >= n_dense) & (unit < n_up))
        def _():
            for copy in up_copies(unit, n_dense, expert_gate, expert_up):
                copy.start()

        @pl.when((unit >= n_up) & (unit < total))
        def _():
            for quarter in range(QUARTERS):
                for copy in down_copies(unit, quarter):
                    copy.start()

    small = [
        pltpu.make_async_copy(source, target, small_sem.at[at])
        for at, (source, target) in enumerate(
            (
                (inputs_hbm, inputs),
                (norm_gain_hbm, norm_gain),
                (ids_hbm, ids),
                (route_hbm, route),
                (out_gain_hbm, out_gain),
            )
        )
    ]
    for copy in small:
        copy.start()
    if n_dense == 0:
        spare_copies = [
            pltpu.make_async_copy(source, spare.at[at], spare_sem.at[at])
            for at, source in enumerate((dense_gate, dense_up))
        ]
        for copy in spare_copies:
            copy.start()
    lax.fori_loop(0, min(slots, total), lambda unit, _: start_unit(unit), None)

    barrier = pltpu.get_barrier_semaphore()

    def greet(offset, _):
        pl.semaphore_signal(barrier, inc=1, device_id={"ep": lax.rem(me + offset, n)})

    lax.fori_loop(1, n, greet, None)

    for copy in small:
        copy.wait()
    value = inputs[...]
    square = jnp.mean(value * value, axis=-1, keepdims=True)
    hidden_own = (value * lax.rsqrt(square + 1e-06) * norm_gain[...]).astype(jnp.bfloat16)
    landed[0] = hidden_own
    pl.semaphore_wait(barrier, n - 1)

    def gather_copy(offset):
        return pltpu.make_async_remote_copy(
            src_ref=landed.at[0],
            dst_ref=landed.at[n - offset],
            send_sem=gather_send.at[offset],
            recv_sem=gather_recv.at[n - offset],
            device_id={"ep": lax.rem(me + offset, n)},
        )

    lax.fori_loop(1, n, lambda offset, _: gather_copy(offset).start(), None)

    weights_all = route[...].astype(jnp.float32) / 1024.0
    named = jnp.sum(jnp.where(ids[...] == expert, weights_all, 0.0), axis=1, keepdims=True)
    zeros = jnp.sum(jnp.where(ids[...] == EXPERTS, weights_all, 0.0), axis=1, keepdims=True)
    named = jnp.broadcast_to(named, (rows, WIDE))
    zeros = jnp.broadcast_to(zeros, (rows, WIDE))
    for block in range(n):
        lines = slice(block * own, (block + 1) * own)
        by_device[0, block] = named[lines]
        by_device[1, block] = zeros[lines]
    for block in range(n):
        scale[block * own : (block + 1) * own] = by_device[0, lax.rem(me + block, n)]
    zero_weight = by_device[1, me][:, :1]

    def landing(offset, _):
        gather_copy(n - offset).wait_recv()

    lax.fori_loop(1, n, landing, None)
    for block in range(n):
        rows_in[block * own : (block + 1) * own] = landed[block]

    def gated(gate, upper):
        return (gate / (1.0 + jnp.exp(-gate)) * upper).astype(jnp.bfloat16)

    def product(left, right):
        return jnp.dot(left, right, preferred_element_type=jnp.float32)

    def up_unit(first, gate_hbm, upper_hbm, hidden):
        def body(unit, _):
            slot = lax.rem(unit, slots)
            copies = up_copies(unit, first, gate_hbm, upper_hbm)
            copies[0].wait()
            gate = product(rows_in[...], ring[slot, 0])
            copies[1].wait()
            upper = product(rows_in[...], ring[slot, 1])
            columns = pl.ds(pl.multiple_of((unit - first) * WIDE, WIDE), WIDE)
            hidden[:, columns] = gated(gate, upper)
            start_unit(unit + slots)

        return body

    if n_dense == 0:
        for copy in spare_copies:
            copy.wait()
        dense_hidden[...] = gated(
            product(rows_in[...], spare[0]), product(rows_in[...], spare[1])
        )
    else:
        lax.fori_loop(0, n_dense, up_unit(0, dense_gate, dense_up, dense_hidden), None)
    lax.fori_loop(n_dense, n_up, up_unit(n_dense, expert_gate, expert_up, expert_hidden), None)

    def reduce_copy(offset, part):
        source, target = outgoing.at[offset], incoming.at[n - offset]
        if part is not None:
            source, target = outgoing.at[offset, part], incoming.at[n - offset, part]
        return pltpu.make_async_remote_copy(
            src_ref=source,
            dst_ref=target,
            send_sem=reduce_send.at[offset],
            recv_sem=reduce_recv.at[n - offset],
            device_id={"ep": lax.rem(me + offset, n)},
        )

    def down_unit(unit, _):
        slot = lax.rem(unit, slots)
        weight = scale[...]
        for quarter in range(QUARTERS):
            for copy in down_copies(unit, quarter):
                copy.wait()
            base = (quarter % 2) * k_both
            block = ring.at[slot, quarter // 2]
            part_sum = product(dense_hidden[...], block[base : base + k_dense])
            part_sum += weight * product(
                expert_hidden[...], block[base + k_dense : base + k_both]
            )
            part = (unit - n_up) * (QUARTERS // 2) + quarter // 2
            side = (quarter % 2) * WIDE
            for to in range(n):
                outgoing[to, part, :, side : side + WIDE] = part_sum[
                    to * own : (to + 1) * own
                ].astype(jnp.bfloat16)
            if quarter % 2 == 1:
                lax.fori_loop(
                    1, n, lambda offset, _: reduce_copy(offset, part).start(), None
                )
        start_unit(unit + slots)

    lax.fori_loop(n_up, total, down_unit, None)

    def arrived(offset, _):
        reduce_copy(n - offset, None).wait_recv()

    lax.fori_loop(1, n, arrived, None)
    parts = []
    chunk = 2 * WIDE
    squares = jnp.zeros((own, 1), jnp.float32)
    for part in range(width // chunk):
        columns = slice(part * chunk, (part + 1) * chunk)
        piece = zero_weight * landed[0, :, columns].astype(jnp.float32)
        piece += outgoing[0, part].astype(jnp.float32)
        for source in range(1, n):
            piece += incoming[source, part].astype(jnp.float32)
        squares += jnp.sum(piece * piece, axis=-1, keepdims=True)
        parts.append(piece)
    factor = lax.rsqrt(squares / width + 1e-06)
    for part, piece in enumerate(parts):
        columns = slice(part * chunk, (part + 1) * chunk)
        out_ref[:, columns] = inputs[:, columns] + piece * factor * out_gain[:, columns]

    def sent(offset, _):
        gather_copy(offset).wait_send()
        reduce_copy(offset, None).wait_send()

    lax.fori_loop(1, n, sent, None)


def on_device(
    inputs,
    norm_gain,
    dense_gate,
    dense_up,
    dense_down,
    expert_gate,
    expert_up,
    expert_down,
    expert_ids,
    route_weights,
    out_gain,
):
    n = lax.axis_size("ep")
    own, width = inputs.shape
    rows = n * own
    cols_dense = dense_gate.shape[1]
    cols_expert = expert_gate.shape[1]
    n_dense = 0 if cols_dense % WIDE else cols_dense // WIDE
    n_expert = cols_expert // WIDE
    n_down = width // (WIDE * QUARTERS)
    spare_shape = (2, width, cols_dense) if n_dense == 0 else (2, 16, 128)
    fixed = 2 * spare_shape[0] * spare_shape[1] * -(-spare_shape[2] // 128) * 128
    fixed += rows * width * 2 * 4 + rows * WIDE * 4 * 8 + 2 * rows * (cols_dense + cols_expert) + (1 << 20)
    slots = min((VMEM_TOTAL - fixed) // (2 * width * WIDE * 2), n_dense + n_expert + n_down)
    cfg = (n, own, slots, n_dense, n_expert, n_down)
    n_parts = width // (2 * WIDE)
    anywhere = pl.BlockSpec(memory_space=pl.ANY)
    return pl.pallas_call(
        functools.partial(kernel, cfg),
        out_shape=jax.ShapeDtypeStruct((own, width), jnp.float32),
        in_specs=[anywhere] * 11,
        out_specs=pl.BlockSpec(memory_space=pltpu.VMEM),
        scratch_shapes=[
            pltpu.VMEM((own, width), jnp.float32),
            pltpu.VMEM((1, width), jnp.float32),
            pltpu.VMEM((1, width), jnp.float32),
            pltpu.VMEM(expert_ids.shape, jnp.int32),
            pltpu.VMEM(route_weights.shape, jnp.int32),
            pltpu.VMEM((slots, 2, width, WIDE), jnp.bfloat16),
            pltpu.VMEM(spare_shape, jnp.bfloat16),
            pltpu.VMEM((n, own, width), jnp.bfloat16),
            pltpu.VMEM((rows, width), jnp.bfloat16),
            pltpu.VMEM((rows, cols_dense), jnp.bfloat16),
            pltpu.VMEM((rows, cols_expert), jnp.bfloat16),
            pltpu.VMEM((2, n, own, WIDE), jnp.float32),
            pltpu.VMEM((rows, WIDE), jnp.float32),
            pltpu.VMEM((n, n_parts, own, 2 * WIDE), jnp.bfloat16),
            pltpu.VMEM((n, n_parts, own, 2 * WIDE), jnp.bfloat16),
            pltpu.SemaphoreType.DMA((5,)),
            pltpu.SemaphoreType.DMA((slots, 2 * QUARTERS)),
            pltpu.SemaphoreType.DMA((2,)),
            pltpu.SemaphoreType.DMA((n,)),
            pltpu.SemaphoreType.DMA((n,)),
            pltpu.SemaphoreType.DMA((n,)),
            pltpu.SemaphoreType.DMA((n,)),
        ],
        compiler_params=pltpu.CompilerParams(
            collective_id=0, has_side_effects=True, vmem_limit_bytes=67_043_328
        ),
        name="layer",
    )(
        inputs,
        norm_gain.reshape(1, width),
        dense_gate,
        dense_up,
        dense_down,
        expert_gate,
        expert_up,
        expert_down,
        expert_ids,
        route_weights,
        out_gain.reshape(1, width),
    )


def solution(mesh):
    placed = (
        P(("groups", "ep"), None),
        P(),
        P(None, "ep"),
        P(None, "ep"),
        P("ep", None),
        P(None, "ep"),
        P(None, "ep"),
        P("ep", None),
        P("groups", None),
        P("groups", None),
        P(),
    )
    return jax.shard_map(
        on_device, mesh=mesh, in_specs=placed, out_specs=P(("groups", "ep"), None), check_vma=False
    )
```

```python
import functools

import jax
import jax.numpy as jnp
from jax import lax
from jax.experimental import pallas as pl
from jax.experimental.pallas import tpu as pltpu
from jax.sharding import PartitionSpec as P

EXPERTS = 16
WIDE = 256
HALVES = 2
LAG = 3
VMEM_TOTAL = 66_000_000


def kernel(
    cfg,
    inputs_hbm,
    norm_gain_hbm,
    dense_gate,
    dense_up,
    dense_down,
    expert_gate,
    expert_up,
    expert_down,
    ids_hbm,
    route_hbm,
    out_gain_hbm,
    out_ref,
    inputs,
    norm_gain,
    out_gain,
    ids,
    route,
    ring,
    spare,
    landed,
    rows_in,
    dense_hidden,
    expert_hidden,
    scale,
    out_near,
    in_near,
    out_far,
    in_far,
    small_sem,
    ring_sem,
    spare_sem,
    gather_send,
    gather_recv,
    near_send,
    near_recv,
    far_send,
    far_recv,
):
    n, near, own, slots, n_dense, n_expert, n_down = cfg
    far = n // near
    rows = n * own
    width = inputs.shape[1]
    k_dense = dense_down.shape[0]
    k_expert = expert_down.shape[0]
    k_both = k_dense + k_expert
    n_up = n_dense + n_expert
    total = n_up + n_down
    me = lax.axis_index("ep")
    expert = me // (n // EXPERTS)
    my_far, my_near = me // near, lax.rem(me, near)

    def to_far(step):
        return {"ep": lax.rem(my_far + step, far) * near + my_near}

    def to_near(step):
        return {"ep": my_far * near + lax.rem(my_near + step, near)}

    def up_copies(unit, first, gate, upper):
        slot = lax.rem(unit, slots)
        columns = pl.ds(pl.multiple_of((unit - first) * WIDE, WIDE), WIDE)
        return [
            pltpu.make_async_copy(
                source.at[:, columns],
                ring.at[slot, :, pl.ds(which * WIDE, WIDE)],
                ring_sem.at[slot, which],
            )
            for which, source in enumerate((gate, upper))
        ]

    def down_copies(unit, half):
        slot = lax.rem(unit, slots)
        start = ((unit - n_up) * HALVES + half) * (2 * WIDE)
        columns = pl.ds(pl.multiple_of(start, 2 * WIDE), 2 * WIDE)
        base = half * k_both
        return [
            pltpu.make_async_copy(
                dense_down.at[:, columns],
                ring.at[slot, pl.ds(base, k_dense)],
                ring_sem.at[slot, 2 * half],
            ),
            pltpu.make_async_copy(
                expert_down.at[:, columns],
                ring.at[slot, pl.ds(base + k_dense, k_expert)],
                ring_sem.at[slot, 2 * half + 1],
            ),
        ]

    def start_unit(unit):
        @pl.when(unit < n_dense)
        def _():
            for copy in up_copies(unit, 0, dense_gate, dense_up):
                copy.start()

        @pl.when((unit >= n_dense) & (unit < n_up))
        def _():
            for copy in up_copies(unit, n_dense, expert_gate, expert_up):
                copy.start()

        @pl.when((unit >= n_up) & (unit < total))
        def _():
            for half in range(HALVES):
                for copy in down_copies(unit, half):
                    copy.start()

    small = [
        pltpu.make_async_copy(source, target, small_sem.at[at])
        for at, (source, target) in enumerate(
            (
                (inputs_hbm, inputs),
                (norm_gain_hbm, norm_gain),
                (ids_hbm, ids),
                (route_hbm, route),
                (out_gain_hbm, out_gain),
            )
        )
    ]
    for copy in small:
        copy.start()
    if n_dense == 0:
        spare_copies = [
            pltpu.make_async_copy(source, spare.at[at], spare_sem.at[at])
            for at, source in enumerate((dense_gate, dense_up))
        ]
        for copy in spare_copies:
            copy.start()
    lax.fori_loop(0, min(slots, total), lambda unit, _: start_unit(unit), None)

    barrier = pltpu.get_barrier_semaphore()

    for step in range(1, far):
        pl.semaphore_signal(barrier, inc=1, device_id=to_far(step))
    for step in range(1, near):
        pl.semaphore_signal(barrier, inc=1, device_id=to_near(step))

    for copy in small:
        copy.wait()
    value = inputs[...]
    square = jnp.mean(value * value, axis=-1, keepdims=True)
    hidden_own = (value * lax.rsqrt(square + 1e-06) * norm_gain[...]).astype(jnp.bfloat16)
    landed[0] = hidden_own
    pl.semaphore_wait(barrier, far + near - 2)

    def gather_far(step):
        return pltpu.make_async_remote_copy(
            src_ref=landed.at[0],
            dst_ref=landed.at[(far - step) * near],
            send_sem=gather_send.at[step * near],
            recv_sem=gather_recv.at[(far - step) * near],
            device_id=to_far(step),
        )

    def gather_near(step, hop):
        return pltpu.make_async_remote_copy(
            src_ref=landed.at[step * near],
            dst_ref=landed.at[step * near + near - hop],
            send_sem=gather_send.at[step * near + hop],
            recv_sem=gather_recv.at[step * near + near - hop],
            device_id=to_near(hop),
        )

    for step in range(1, far):
        gather_far(step).start()
    for hop in range(1, near):
        gather_near(0, hop).start()

    weights_all = route[...].astype(jnp.float32) / 1024.0
    named = jnp.sum(jnp.where(ids[...] == expert, weights_all, 0.0), axis=0, keepdims=True)
    zeros = jnp.sum(jnp.where(ids[...] == EXPERTS, weights_all, 0.0), axis=0, keepdims=True)
    line = lax.broadcasted_iota(jnp.int32, (rows, rows), 0)
    block, inside = line // own, lax.rem(line, own)
    source_far = lax.rem(my_far + block // near, far)
    source_near = lax.rem(my_near + lax.rem(block, near), near)
    source = (source_far * near + source_near) * own + inside
    column = lax.broadcasted_iota(jnp.int32, (rows, rows), 1)
    weight = jnp.sum(jnp.where(column == source, named, 0.0), axis=1, keepdims=True)
    scale[...] = jnp.broadcast_to(weight, scale.shape)
    own_line = lax.broadcasted_iota(jnp.int32, (own, rows), 0) + me * own
    own_column = lax.broadcasted_iota(jnp.int32, (own, rows), 1)
    zero_weight = jnp.sum(jnp.where(own_column == own_line, zeros, 0.0), axis=1, keepdims=True)

    def place(block):
        rows_in[block * own : (block + 1) * own] = landed[block]

    place(0)
    for step in range(1, far):
        gather_far(far - step).wait_recv()
        for hop in range(1, near):
            gather_near(step, hop).start()
        place(step * near)
    for step in range(far):
        for hop in range(1, near):
            gather_near(step, near - hop).wait_recv()
            place(step * near + hop)

    def gated(gate, upper):
        return (gate / (1.0 + jnp.exp(-gate)) * upper).astype(jnp.bfloat16)

    def product(left, right):
        return jnp.dot(left, right, preferred_element_type=jnp.float32)

    def up_unit(first, gate_hbm, upper_hbm, hidden):
        def body(unit, _):
            slot = lax.rem(unit, slots)
            copies = up_copies(unit, first, gate_hbm, upper_hbm)
            for copy in copies:
                copy.wait()
            both = product(rows_in[...], ring[slot])
            gate, upper = both[:, :WIDE], both[:, WIDE:]
            columns = pl.ds(pl.multiple_of((unit - first) * WIDE, WIDE), WIDE)
            hidden[:, columns] = gated(gate, upper)
            start_unit(unit + slots)

        return body

    if n_dense == 0:
        for copy in spare_copies:
            copy.wait()
        dense_hidden[...] = gated(
            product(rows_in[...], spare[0]), product(rows_in[...], spare[1])
        )
    else:
        lax.fori_loop(0, n_dense, up_unit(0, dense_gate, dense_up, dense_hidden), None)
    lax.fori_loop(n_dense, n_up, up_unit(n_dense, expert_gate, expert_up, expert_hidden), None)

    n_parts = width // (2 * WIDE)

    def near_copy(hop, part):
        source, target = out_near.at[hop], in_near.at[near - hop]
        if part is not None:
            source, target = out_near.at[hop, part], in_near.at[near - hop, part]
        return pltpu.make_async_remote_copy(
            src_ref=source,
            dst_ref=target,
            send_sem=near_send.at[hop],
            recv_sem=near_recv.at[near - hop, 0 if part is None else part],
            device_id=to_near(hop),
        )

    def far_copy(step, part):
        source, target = out_far.at[step], in_far.at[far - step]
        if part is not None:
            source, target = out_far.at[step, part], in_far.at[far - step, part]
        return pltpu.make_async_remote_copy(
            src_ref=source,
            dst_ref=target,
            send_sem=far_send.at[step],
            recv_sem=far_recv.at[far - step],
            device_id=to_far(step),
        )

    def pass_on(part):
        for hop in range(1, near):
            near_copy(near - hop, part).wait_recv()
        for step in range(far):
            piece = out_near[0, part, step].astype(jnp.float32)
            for hop in range(1, near):
                piece += in_near[hop, part, step].astype(jnp.float32)
            out_far[step, part] = piece.astype(out_far.dtype)
        for step in range(1, far):
            far_copy(step, part).start()

    def down_unit(unit, _):
        slot = lax.rem(unit, slots)
        weight = scale[...]
        for half in range(HALVES):
            for copy in down_copies(unit, half):
                copy.wait()
            base = half * k_both
            block = ring.at[slot]
            part_sum = product(dense_hidden[...], block[base : base + k_dense])
            part_sum += weight * product(
                expert_hidden[...], block[base + k_dense : base + k_both]
            )
            part = (unit - n_up) * HALVES + half
            for to in range(n):
                out_near[to % near, part, to // near] = part_sum[
                    to * own : (to + 1) * own
                ].astype(jnp.bfloat16)
            for hop in range(1, near):
                near_copy(hop, part).start()

            @pl.when(part >= LAG)
            def _():
                pass_on(part - LAG)

        start_unit(unit + slots)

    lax.fori_loop(n_up, total, down_unit, None)

    lax.fori_loop(n_parts - LAG, n_parts, lambda part, _: pass_on(part), None)
    for step in range(1, far):
        far_copy(far - step, None).wait_recv()
    parts = []
    chunk = 2 * WIDE
    squares = jnp.zeros((own, 1), jnp.float32)
    for part in range(width // chunk):
        columns = slice(part * chunk, (part + 1) * chunk)
        piece = zero_weight * landed[0, :, columns].astype(jnp.float32)
        piece += out_far[0, part].astype(jnp.float32)
        for step in range(1, far):
            piece += in_far[step, part].astype(jnp.float32)
        squares += jnp.sum(piece * piece, axis=-1, keepdims=True)
        parts.append(piece)
    factor = lax.rsqrt(squares / width + 1e-06)
    for part, piece in enumerate(parts):
        columns = slice(part * chunk, (part + 1) * chunk)
        out_ref[:, columns] = inputs[:, columns] + piece * factor * out_gain[:, columns]

    for step in range(1, far):
        gather_far(step).wait_send()
        far_copy(step, None).wait_send()
    for hop in range(1, near):
        for step in range(far):
            gather_near(step, hop).wait_send()
        near_copy(hop, None).wait_send()


def on_device(
    inputs,
    norm_gain,
    dense_gate,
    dense_up,
    dense_down,
    expert_gate,
    expert_up,
    expert_down,
    expert_ids,
    route_weights,
    out_gain,
):
    n = lax.axis_size("ep")
    own, width = inputs.shape
    rows = n * own
    cols_dense = dense_gate.shape[1]
    cols_expert = expert_gate.shape[1]
    n_dense = 0 if cols_dense % WIDE else cols_dense // WIDE
    n_expert = cols_expert // WIDE
    n_down = width // (2 * WIDE * HALVES)
    spare_shape = (2, width, cols_dense) if n_dense == 0 else (2, 16, 128)
    fixed = 2 * spare_shape[0] * spare_shape[1] * -(-spare_shape[2] // 128) * 128
    fixed += rows * width * 2 * 4 + rows * WIDE * 4 * 8 + 2 * rows * (cols_dense + cols_expert) + (1 << 20)
    slots = min((VMEM_TOTAL - fixed) // (2 * width * WIDE * 2), n_dense + n_expert + n_down)
    near = 1
    while near * near < n:
        near *= 2
    far = n // near
    cfg = (n, near, own, slots, n_dense, n_expert, n_down)
    n_parts = width // (2 * WIDE)
    anywhere = pl.BlockSpec(memory_space=pl.ANY)
    return pl.pallas_call(
        functools.partial(kernel, cfg),
        out_shape=jax.ShapeDtypeStruct((own, width), jnp.float32),
        in_specs=[anywhere] * 11,
        out_specs=pl.BlockSpec(memory_space=pltpu.VMEM),
        scratch_shapes=[
            pltpu.VMEM((own, width), jnp.float32),
            pltpu.VMEM((1, width), jnp.float32),
            pltpu.VMEM((1, width), jnp.float32),
            pltpu.VMEM(expert_ids.shape[::-1], jnp.int32),
            pltpu.VMEM(route_weights.shape[::-1], jnp.int32),
            pltpu.VMEM((slots, width, 2 * WIDE), jnp.bfloat16),
            pltpu.VMEM(spare_shape, jnp.bfloat16),
            pltpu.VMEM((n, own, width), jnp.bfloat16),
            pltpu.VMEM((rows, width), jnp.bfloat16),
            pltpu.VMEM((rows, cols_dense), jnp.bfloat16),
            pltpu.VMEM((rows, cols_expert), jnp.bfloat16),
            pltpu.VMEM((rows, 2 * WIDE), jnp.float32),
            pltpu.VMEM((near, n_parts, far, own, 2 * WIDE), jnp.bfloat16),
            pltpu.VMEM((near, n_parts, far, own, 2 * WIDE), jnp.bfloat16),
            pltpu.VMEM((far, n_parts, own, 2 * WIDE), jnp.bfloat16),
            pltpu.VMEM((far, n_parts, own, 2 * WIDE), jnp.bfloat16),
            pltpu.SemaphoreType.DMA((5,)),
            pltpu.SemaphoreType.DMA((slots, 2 * HALVES)),
            pltpu.SemaphoreType.DMA((2,)),
            pltpu.SemaphoreType.DMA((n,)),
            pltpu.SemaphoreType.DMA((n,)),
            pltpu.SemaphoreType.DMA((near,)),
            pltpu.SemaphoreType.DMA((near, n_parts)),
            pltpu.SemaphoreType.DMA((far,)),
            pltpu.SemaphoreType.DMA((far,)),
        ],
        compiler_params=pltpu.CompilerParams(
            collective_id=0, has_side_effects=True, vmem_limit_bytes=67_043_328
        ),
        name="layer",
    )(
        inputs,
        norm_gain.reshape(1, width),
        dense_gate,
        dense_up,
        dense_down,
        expert_gate,
        expert_up,
        expert_down,
        expert_ids.T,
        route_weights.T,
        out_gain.reshape(1, width),
    )


def solution(mesh):
    placed = (
        P(("groups", "ep"), None),
        P(),
        P(None, "ep"),
        P(None, "ep"),
        P("ep", None),
        P(None, "ep"),
        P(None, "ep"),
        P("ep", None),
        P("groups", None),
        P("groups", None),
        P(),
    )
    return jax.shard_map(
        on_device, mesh=mesh, in_specs=placed, out_specs=P(("groups", "ep"), None), check_vma=False
    )
```

```python
import functools

import jax
import jax.numpy as jnp
from jax import lax
from jax.experimental import pallas as pl
from jax.experimental.pallas import tpu as pltpu
from jax.sharding import PartitionSpec as P

EXPERTS = 16
WIDE = 256
HALVES = 2
DIRECT = 2
LAG = 3
VMEM_TOTAL = 66_000_000


def kernel(
    cfg,
    inputs_hbm,
    norm_gain_hbm,
    dense_gate,
    dense_up,
    dense_down,
    expert_gate,
    expert_up,
    expert_down,
    ids_hbm,
    route_hbm,
    out_gain_hbm,
    out_ref,
    inputs,
    norm_gain,
    out_gain,
    ids,
    route,
    ring,
    spare,
    landed,
    rows_in,
    dense_hidden,
    expert_hidden,
    scale,
    out_near,
    in_near,
    out_far,
    in_far,
    out_direct,
    in_direct,
    small_sem,
    ring_sem,
    spare_sem,
    gather_send,
    gather_recv,
    near_send,
    near_recv,
    far_send,
    far_recv,
    direct_send,
    direct_recv,
):
    n, near, own, slots, n_dense, n_expert, n_down = cfg
    far = n // near
    rows = n * own
    width = inputs.shape[1]
    k_dense = dense_down.shape[0]
    k_expert = expert_down.shape[0]
    k_both = k_dense + k_expert
    n_up = n_dense + n_expert
    total = n_up + n_down
    me = lax.axis_index("ep")
    expert = me // (n // EXPERTS)
    my_far, my_near = me // near, lax.rem(me, near)

    def to_far(step):
        return {"ep": lax.rem(my_far + step, far) * near + my_near}

    def to_near(step):
        return {"ep": my_far * near + lax.rem(my_near + step, near)}

    def up_copies(unit, first, gate, upper):
        slot = lax.rem(unit, slots)
        columns = pl.ds(pl.multiple_of((unit - first) * WIDE, WIDE), WIDE)
        return [
            pltpu.make_async_copy(
                source.at[:, columns],
                ring.at[slot, :, pl.ds(which * WIDE, WIDE)],
                ring_sem.at[slot, which],
            )
            for which, source in enumerate((gate, upper))
        ]

    def down_copies(unit, half):
        slot = lax.rem(unit, slots)
        start = ((unit - n_up) * HALVES + half) * (2 * WIDE)
        columns = pl.ds(pl.multiple_of(start, 2 * WIDE), 2 * WIDE)
        base = half * k_both
        return [
            pltpu.make_async_copy(
                dense_down.at[:, columns],
                ring.at[slot, pl.ds(base, k_dense)],
                ring_sem.at[slot, 2 * half],
            ),
            pltpu.make_async_copy(
                expert_down.at[:, columns],
                ring.at[slot, pl.ds(base + k_dense, k_expert)],
                ring_sem.at[slot, 2 * half + 1],
            ),
        ]

    def start_unit(unit):
        @pl.when(unit < n_dense)
        def _():
            for copy in up_copies(unit, 0, dense_gate, dense_up):
                copy.start()

        @pl.when((unit >= n_dense) & (unit < n_up))
        def _():
            for copy in up_copies(unit, n_dense, expert_gate, expert_up):
                copy.start()

        @pl.when((unit >= n_up) & (unit < total))
        def _():
            for half in range(HALVES):
                for copy in down_copies(unit, half):
                    copy.start()

    small = [
        pltpu.make_async_copy(source, target, small_sem.at[at])
        for at, (source, target) in enumerate(
            (
                (inputs_hbm, inputs),
                (norm_gain_hbm, norm_gain),
                (ids_hbm, ids),
                (route_hbm, route),
                (out_gain_hbm, out_gain),
            )
        )
    ]
    for copy in small:
        copy.start()
    if n_dense == 0:
        spare_copies = [
            pltpu.make_async_copy(source, spare.at[at], spare_sem.at[at])
            for at, source in enumerate((dense_gate, dense_up))
        ]
        for copy in spare_copies:
            copy.start()
    lax.fori_loop(0, min(slots, total), lambda unit, _: start_unit(unit), None)

    barrier = pltpu.get_barrier_semaphore()

    def greet(offset, _):
        pl.semaphore_signal(barrier, inc=1, device_id={"ep": lax.rem(me + offset, n)})

    lax.fori_loop(1, n, greet, None)

    for copy in small:
        copy.wait()
    value = inputs[...]
    square = jnp.mean(value * value, axis=-1, keepdims=True)
    hidden_own = (value * lax.rsqrt(square + 1e-06) * norm_gain[...]).astype(jnp.bfloat16)
    landed[0] = hidden_own
    pl.semaphore_wait(barrier, n - 1)

    def gather_far(step):
        return pltpu.make_async_remote_copy(
            src_ref=landed.at[0],
            dst_ref=landed.at[(far - step) * near],
            send_sem=gather_send.at[step * near],
            recv_sem=gather_recv.at[(far - step) * near],
            device_id=to_far(step),
        )

    def gather_near(step, hop):
        return pltpu.make_async_remote_copy(
            src_ref=landed.at[step * near],
            dst_ref=landed.at[step * near + near - hop],
            send_sem=gather_send.at[step * near + hop],
            recv_sem=gather_recv.at[step * near + near - hop],
            device_id=to_near(hop),
        )

    for step in range(1, far):
        gather_far(step).start()
    for hop in range(1, near):
        gather_near(0, hop).start()

    weights_all = route[...].astype(jnp.float32) / 1024.0
    named = jnp.sum(jnp.where(ids[...] == expert, weights_all, 0.0), axis=0, keepdims=True)
    zeros = jnp.sum(jnp.where(ids[...] == EXPERTS, weights_all, 0.0), axis=0, keepdims=True)
    line = lax.broadcasted_iota(jnp.int32, (rows, rows), 0)
    block, inside = line // own, lax.rem(line, own)
    source_far = lax.rem(my_far + block // near, far)
    source_near = lax.rem(my_near + lax.rem(block, near), near)
    source = (source_far * near + source_near) * own + inside
    column = lax.broadcasted_iota(jnp.int32, (rows, rows), 1)
    weight = jnp.sum(jnp.where(column == source, named, 0.0), axis=1, keepdims=True)
    scale[...] = jnp.broadcast_to(weight, scale.shape)
    own_line = lax.broadcasted_iota(jnp.int32, (own, rows), 0) + me * own
    own_column = lax.broadcasted_iota(jnp.int32, (own, rows), 1)
    zero_weight = jnp.sum(jnp.where(own_column == own_line, zeros, 0.0), axis=1, keepdims=True)

    def place(block):
        rows_in[block * own : (block + 1) * own] = landed[block]

    place(0)
    for step in range(1, far):
        gather_far(far - step).wait_recv()
        for hop in range(1, near):
            gather_near(step, hop).start()
        place(step * near)
    for step in range(far):
        for hop in range(1, near):
            gather_near(step, near - hop).wait_recv()
            place(step * near + hop)

    def gated(gate, upper):
        return (gate / (1.0 + jnp.exp(-gate)) * upper).astype(jnp.bfloat16)

    def product(left, right):
        return jnp.dot(left, right, preferred_element_type=jnp.float32)

    def up_unit(first, gate_hbm, upper_hbm, hidden):
        def body(unit, _):
            slot = lax.rem(unit, slots)
            copies = up_copies(unit, first, gate_hbm, upper_hbm)
            for copy in copies:
                copy.wait()
            both = product(rows_in[...], ring[slot])
            gate, upper = both[:, :WIDE], both[:, WIDE:]
            columns = pl.ds(pl.multiple_of((unit - first) * WIDE, WIDE), WIDE)
            hidden[:, columns] = gated(gate, upper)
            start_unit(unit + slots)

        return body

    if n_dense == 0:
        for copy in spare_copies:
            copy.wait()
        dense_hidden[...] = gated(
            product(rows_in[...], spare[0]), product(rows_in[...], spare[1])
        )
    else:
        lax.fori_loop(0, n_dense, up_unit(0, dense_gate, dense_up, dense_hidden), None)
    lax.fori_loop(n_dense, n_up, up_unit(n_dense, expert_gate, expert_up, expert_hidden), None)

    n_parts = width // (2 * WIDE)
    n_hops = n_parts - DIRECT * HALVES

    def direct_copy(block, part):
        there_far, there_near = block // near, lax.rem(block, near)
        back = lax.rem(far - there_far, far) * near + lax.rem(near - there_near, near)
        source, target = out_direct.at[block], in_direct.at[back]
        if part is not None:
            source, target = out_direct.at[block, part], in_direct.at[back, part]
        to = lax.rem(my_far + there_far, far) * near + lax.rem(my_near + there_near, near)
        return pltpu.make_async_remote_copy(
            src_ref=source,
            dst_ref=target,
            send_sem=direct_send.at[block],
            recv_sem=direct_recv.at[back],
            device_id={"ep": to},
        )

    def near_copy(hop, part):
        source, target = out_near.at[hop], in_near.at[near - hop]
        if part is not None:
            source, target = out_near.at[hop, part], in_near.at[near - hop, part]
        return pltpu.make_async_remote_copy(
            src_ref=source,
            dst_ref=target,
            send_sem=near_send.at[hop],
            recv_sem=near_recv.at[near - hop, 0 if part is None else part],
            device_id=to_near(hop),
        )

    def far_copy(step, part):
        source, target = out_far.at[step], in_far.at[far - step]
        if part is not None:
            source, target = out_far.at[step, part], in_far.at[far - step, part]
        return pltpu.make_async_remote_copy(
            src_ref=source,
            dst_ref=target,
            send_sem=far_send.at[step],
            recv_sem=far_recv.at[far - step],
            device_id=to_far(step),
        )

    def pass_on(part):
        for hop in range(1, near):
            near_copy(near - hop, part).wait_recv()
        for step in range(far):
            piece = out_near[0, part, step].astype(jnp.float32)
            for hop in range(1, near):
                piece += in_near[hop, part, step].astype(jnp.float32)
            out_far[step, part] = piece.astype(out_far.dtype)
        for step in range(1, far):
            far_copy(step, part).start()

    def down_unit(unit, _):
        slot = lax.rem(unit, slots)
        weight = scale[...]
        for half in range(HALVES):
            for copy in down_copies(unit, half):
                copy.wait()
            base = half * k_both
            block = ring.at[slot]
            part_sum = product(dense_hidden[...], block[base : base + k_dense])
            part_sum += weight * product(
                expert_hidden[...], block[base + k_dense : base + k_both]
            )
            part = (unit - n_up) * HALVES + half
            for to in range(n):
                out_near[to % near, part, to // near] = part_sum[
                    to * own : (to + 1) * own
                ].astype(jnp.bfloat16)
            for hop in range(1, near):
                near_copy(hop, part).start()

            @pl.when(part >= LAG)
            def _():
                pass_on(part - LAG)

        start_unit(unit + slots)

    def direct_unit(unit, _):
        slot = lax.rem(unit, slots)
        weight = scale[...]
        for half in range(HALVES):
            for copy in down_copies(unit, half):
                copy.wait()
            base = half * k_both
            block = ring.at[slot]
            part_sum = product(dense_hidden[...], block[base : base + k_dense])
            part_sum += weight * product(
                expert_hidden[...], block[base + k_dense : base + k_both]
            )
            part = (unit - n_up) * HALVES + half
            for to in range(n):
                out_direct[to, part - n_hops] = part_sum[to * own : (to + 1) * own].astype(
                    jnp.bfloat16
                )
            lax.fori_loop(
                1, n, lambda block, _: direct_copy(block, part - n_hops).start(), None
            )

            @pl.when(part - LAG < n_hops)
            def _():
                pass_on(part - LAG)

        start_unit(unit + slots)

    lax.fori_loop(n_up, total - DIRECT, down_unit, None)
    lax.fori_loop(total - DIRECT, total, direct_unit, None)

    for step in range(1, far):
        far_copy(far - step, None).wait_recv()

    def landed_direct(block, _):
        direct_copy(block, None).wait_recv()

    def sent_direct(block, _):
        direct_copy(block, None).wait_send()

    parts = []
    chunk = 2 * WIDE
    squares = jnp.zeros((own, 1), jnp.float32)
    for part in range(width // chunk):
        columns = slice(part * chunk, (part + 1) * chunk)
        piece = zero_weight * landed[0, :, columns].astype(jnp.float32)
        if part == n_hops:
            lax.fori_loop(1, n, landed_direct, None)
        own_part, others, at = out_far, in_far, part
        if part >= n_hops:
            own_part, others, at = out_direct, in_direct, part - n_hops
        piece += own_part[0, at].astype(jnp.float32)
        for step in range(1, others.shape[0]):
            piece += others[step, at].astype(jnp.float32)
        squares += jnp.sum(piece * piece, axis=-1, keepdims=True)
        parts.append(piece)
    factor = lax.rsqrt(squares / width + 1e-06)
    for part, piece in enumerate(parts):
        columns = slice(part * chunk, (part + 1) * chunk)
        out_ref[:, columns] = inputs[:, columns] + piece * factor * out_gain[:, columns]

    for step in range(1, far):
        gather_far(step).wait_send()
        far_copy(step, None).wait_send()
    for hop in range(1, near):
        for step in range(far):
            gather_near(step, hop).wait_send()
        near_copy(hop, None).wait_send()
    lax.fori_loop(1, n, sent_direct, None)


def on_device(
    inputs,
    norm_gain,
    dense_gate,
    dense_up,
    dense_down,
    expert_gate,
    expert_up,
    expert_down,
    expert_ids,
    route_weights,
    out_gain,
):
    n = lax.axis_size("ep")
    own, width = inputs.shape
    rows = n * own
    cols_dense = dense_gate.shape[1]
    cols_expert = expert_gate.shape[1]
    n_dense = 0 if cols_dense % WIDE else cols_dense // WIDE
    n_expert = cols_expert // WIDE
    n_down = width // (2 * WIDE * HALVES)
    spare_shape = (2, width, cols_dense) if n_dense == 0 else (2, 16, 128)
    fixed = 2 * spare_shape[0] * spare_shape[1] * -(-spare_shape[2] // 128) * 128
    fixed += rows * width * 2 * 4 + rows * WIDE * 4 * 8 + 2 * rows * (cols_dense + cols_expert) + (1 << 20)
    slots = min((VMEM_TOTAL - fixed) // (2 * width * WIDE * 2), n_dense + n_expert + n_down)
    near = 1
    while near * near < n:
        near *= 2
    far = n // near
    cfg = (n, near, own, slots, n_dense, n_expert, n_down)
    n_parts = width // (2 * WIDE)
    n_hops = n_parts - DIRECT * HALVES
    anywhere = pl.BlockSpec(memory_space=pl.ANY)
    return pl.pallas_call(
        functools.partial(kernel, cfg),
        out_shape=jax.ShapeDtypeStruct((own, width), jnp.float32),
        in_specs=[anywhere] * 11,
        out_specs=pl.BlockSpec(memory_space=pltpu.VMEM),
        scratch_shapes=[
            pltpu.VMEM((own, width), jnp.float32),
            pltpu.VMEM((1, width), jnp.float32),
            pltpu.VMEM((1, width), jnp.float32),
            pltpu.VMEM(expert_ids.shape[::-1], jnp.int32),
            pltpu.VMEM(route_weights.shape[::-1], jnp.int32),
            pltpu.VMEM((slots, width, 2 * WIDE), jnp.bfloat16),
            pltpu.VMEM(spare_shape, jnp.bfloat16),
            pltpu.VMEM((n, own, width), jnp.bfloat16),
            pltpu.VMEM((rows, width), jnp.bfloat16),
            pltpu.VMEM((rows, cols_dense), jnp.bfloat16),
            pltpu.VMEM((rows, cols_expert), jnp.bfloat16),
            pltpu.VMEM((rows, 2 * WIDE), jnp.float32),
            pltpu.VMEM((near, n_hops, far, own, 2 * WIDE), jnp.bfloat16),
            pltpu.VMEM((near, n_hops, far, own, 2 * WIDE), jnp.bfloat16),
            pltpu.VMEM((far, n_hops, own, 2 * WIDE), jnp.bfloat16),
            pltpu.VMEM((far, n_hops, own, 2 * WIDE), jnp.bfloat16),
            pltpu.VMEM((n, n_parts - n_hops, own, 2 * WIDE), jnp.bfloat16),
            pltpu.VMEM((n, n_parts - n_hops, own, 2 * WIDE), jnp.bfloat16),
            pltpu.SemaphoreType.DMA((5,)),
            pltpu.SemaphoreType.DMA((slots, 2 * HALVES)),
            pltpu.SemaphoreType.DMA((2,)),
            pltpu.SemaphoreType.DMA((n,)),
            pltpu.SemaphoreType.DMA((n,)),
            pltpu.SemaphoreType.DMA((near,)),
            pltpu.SemaphoreType.DMA((near, n_hops)),
            pltpu.SemaphoreType.DMA((far,)),
            pltpu.SemaphoreType.DMA((far,)),
            pltpu.SemaphoreType.DMA((n,)),
            pltpu.SemaphoreType.DMA((n,)),
        ],
        compiler_params=pltpu.CompilerParams(
            collective_id=0, has_side_effects=True, vmem_limit_bytes=67_043_328
        ),
        name="layer",
    )(
        inputs,
        norm_gain.reshape(1, width),
        dense_gate,
        dense_up,
        dense_down,
        expert_gate,
        expert_up,
        expert_down,
        expert_ids.T,
        route_weights.T,
        out_gain.reshape(1, width),
    )


def solution(mesh):
    placed = (
        P(("groups", "ep"), None),
        P(),
        P(None, "ep"),
        P(None, "ep"),
        P("ep", None),
        P(None, "ep"),
        P(None, "ep"),
        P("ep", None),
        P("groups", None),
        P("groups", None),
        P(),
    )
    return jax.shard_map(
        on_device, mesh=mesh, in_specs=placed, out_specs=P(("groups", "ep"), None), check_vma=False
    )
```
